32 devices in a mesh: parts: 2 (over y), expert: 8 (over z, x), group: 1, tensor: 2 (over core).
Axes of the slice: x: 2, y: 2, z: 4, core: 2. Of those that a mesh axis runs over, the one named last changes fastest.
Arguments:
- hidden_in: bfloat16 [3, 64, 4096], P(None, ('parts', 'expert', 'group')), parts along dimension 1, may hold values from -6 to 6
- queries: bfloat16 [3, 64, 32, 128], P(None, ('parts', 'expert', 'group'), 'tensor'), parts along dimension 1, may hold values from -32 to 32
- new_keys: bfloat16 [3, 64, 4, 128], P(None, ('parts', 'expert', 'group'), 'tensor'), parts along dimension 1, may hold values from -4 to 4
- new_values: bfloat16 [3, 64, 4, 128], P(None, ('parts', 'expert', 'group'), 'tensor'), parts along dimension 1, may hold values from -8 to 8
- cache_keys: bfloat16 [64, 4, 128, 128], P(('parts', 'expert', 'group'), 'tensor'), parts along dimension 0, may hold values from -4 to 4
- cache_values: bfloat16 [64, 4, 128, 128], P(('parts', 'expert', 'group'), 'tensor'), parts along dimension 0, may hold values from -8 to 8
- route_ids: int32 [3, 64, 8], P(None, ('parts', 'expert', 'group')), parts along dimension 1, may hold values from 0 to 15, all different within a row; in each aligned block of 4 rows (0 to 3, 4 to 7, ..., all dimensions but the last counted through in order) at most 4 rows name the same one
- route_weights: float32 [3, 64, 8], P(None, ('parts', 'expert', 'group')), parts along dimension 1, may hold values from 0.1 to 1
- norm_gain: float32 [4096], replicated, may hold values from 0.25 to 1.75
- gate_weight: bfloat16 [16, 4096, 768], P('expert', 'group', 'tensor'), may hold values from -0.09375 to 0.09375
- up_weight: bfloat16 [16, 4096, 768], P('expert', 'group', 'tensor'), may hold values from -0.09375 to 0.09375
- down_weight: bfloat16 [16, 768, 4096], P('expert', None, ('group', 'tensor')), may hold values from -0.21875 to 0.21875
- ancestor_counts: int32 [64], P(('parts', 'expert', 'group')), parts along dimension 0, may hold values from 0 to 5, as said below
Outputs:
- layer_out: bfloat16 [3, 64, 4096], P(None, ('parts', 'expert', 'group')), parts along dimension 1
- resampled_keys: bfloat16 [64, 4, 131, 128], P(('parts', 'expert', 'group'), 'tensor'), parts along dimension 0
- resampled_values: bfloat16 [64, 4, 131, 128], P(('parts', 'expert', 'group'), 'tensor'), parts along dimension 0
The draws below stay inside these ranges and needn't reach their ends.
There are 2 independent parts, one for each index of `parts`. The reference program is written for one: setup_inputs(seed, part) draws one part's arguments, and reference() takes and returns one part's arrays. A program takes and returns all parts, laid end to end along the dimension named above; an argument that names none is the same for every part. Nothing has to cross between parts.
Inputs may be any that keep to these rules, and one draw needn't show every extreme that they name: `route_ids`: each row names 8 different experts; in each aligned block of 4 rows (the rows of one device in one step) no expert is named by more than 4 rows. `ancestor_counts`: the counts sum to 32, and every particle i descends from a particle within 2 positions of i.
All inputs are finite; a program needn't handle non-finite values.
Results may differ from the reference program's by a relative error of at most 0.0075.
Values may be sent and summed in bfloat16 or wider, within the bound.
A program may use at most 64 MiB of HBM per device.

```python
import math
import jax
import jax.numpy as jnp
import numpy as np
from jax import lax

D = 4096
FF = 768
QH = 32
KVH = 4
HD = 128
TOPK = 8
STEPS = 3
REACH = 2
TOK_DEV = 4
CACHE = 128
EXPERTS = 16
PARTICLES = 32
CAP = 4
N_GROUP = 1


def drawn_pair(key):
    cached = jnp.clip(jax.random.normal(jax.random.fold_in(key, 41), (PARTICLES, KVH, CACHE, HD), jnp.float32), -4.0, 4.0)
    queries_drawn = jnp.clip(jax.random.normal(jax.random.fold_in(key, 42), (STEPS, PARTICLES, QH, HD), jnp.float32), -4.0, 4.0)
    return (queries_drawn, cached)


def draw_queries(key, part):
    return drawn_pair(key)[0].astype(jnp.bfloat16)


def draw_cache_keys(key, part):
    return drawn_pair(key)[1].astype(jnp.bfloat16)


def draw_ancestor_counts(key, part):
    indices = jnp.arange(PARTICLES, dtype=jnp.int32)
    offsets = jax.random.randint(jax.random.fold_in(key, 51), (PARTICLES,), -REACH, REACH + 1, dtype=jnp.int32)
    marked = jax.random.randint(jax.random.fold_in(key, 52), (), 0, PARTICLES - REACH, dtype=jnp.int32)
    offsets = jnp.where(indices == marked, REACH, offsets)
    before_edge = (indices >= TOK_DEV - 2 * REACH) & (indices < TOK_DEV)
    offsets = jnp.where(before_edge, jnp.minimum(offsets, TOK_DEV - REACH - indices), offsets)
    offsets = jnp.where(indices == TOK_DEV, -REACH, offsets)
    ancestor = lax.cummax(jnp.clip(indices + offsets, 0, PARTICLES - 1), axis=0)
    return jnp.sum((ancestor[:, None] == indices[None, :]).astype(jnp.int32), axis=0)


def steps_of(rng, shape, split, smallest, top_value):
    def one(dim, parts):
        draws = jax.random.uniform(jax.random.fold_in(jax.random.fold_in(rng, 6), dim), (parts,), jnp.float32, smallest / len(split), top_value / len(split))
        return jnp.repeat(jnp.exp(draws), shape[dim] // parts).reshape((-1,) + (1,) * (len(shape) - dim - 1))

    factor_of = one(*split[0])
    for cut in split[1:]:
        factor_of = factor_of * one(*cut)
    return factor_of


def assign_block(stream_key, own, number, rows, count, top, most, skew):
    order = jax.random.permutation(stream_key, count)
    crowded, usual = portions_of(count, rows * top, most, skew, True), portions_of(count, rows * top, most, skew, False)
    places = jnp.arange(count)

    def named(lengths, rotation):
        used = int((lengths > 0).sum())
        fixed = max(1, used // 4)
        passed = fixed + (places - fixed + rotation * (used - fixed)) % max(1, count - fixed)
        return jnp.zeros((count,), jnp.int32).at[order[jnp.where(places < fixed, places, passed)]].set(jnp.asarray(lengths, jnp.int32))

    lengths = jnp.where(number % 4 == 0, named(crowded, number // 4), named(usual, number - number // 4 - 1))
    mixed = jax.random.permutation(jax.random.fold_in(own, 3), count)
    giver, receiver = mixed[0:count // 2 * 2:2], mixed[1:count // 2 * 2:2]
    slack = jnp.minimum(lengths[giver] - 1, most - lengths[receiver]) // 2
    slack = jnp.where((giver == order[0]) | (receiver == order[0]) | (lengths[receiver] == 0), 0, jnp.maximum(slack, 0))
    passed = jax.random.randint(jax.random.fold_in(own, 4), (count // 2,), 0, 1 << 20) % (slack + 1)
    lengths = lengths.at[giver].add(-passed).at[receiver].add(passed)
    labels = jnp.searchsorted(jnp.cumsum(lengths), jnp.arange(rows * top), side="right").astype(jnp.int32)
    listing = labels.reshape(top, rows).T
    listing = listing[jax.random.permutation(jax.random.fold_in(own, 1), rows)]
    rotation = jax.random.randint(jax.random.fold_in(own, 2), (rows, 1), 0, top)
    return jnp.take_along_axis(listing, (jnp.arange(top)[None, :] + rotation) % top, axis=1)


def portions_of(count, total, limit, slope, full):
    weights = [(1 << 20) // math.isqrt(rank ** slope) + 1 for rank in range(1, count + 1)]
    largest = limit if full else min(limit, max(-(-total // count), total * weights[0] // sum(weights)))
    least = 1 if total - largest >= count - 1 else 0
    holding, spare = [largest] + [least] * (count - 1), total - largest - least * (count - 1)
    while spare > 0:
        free = [i for i in range(1, count) if holding[i] < largest] or [i for i in range(1, count) if holding[i] < limit]
        mass, left = sum([weights[i] for i in free]), spare
        for i in free:
            addition = min(limit - holding[i], max(1, left * weights[i] // mass), spare)
            holding[i] = holding[i] + addition
            spare = spare - addition
    return np.array(holding)


def normal_values(stream_key, dims, deviation, limit, pieces=(), kind=jnp.bfloat16):
    entries = deviation * jax.random.normal(stream_key, dims, jnp.float32)
    if pieces:
        entries = entries * steps_of(stream_key, dims, pieces, -0.22, 0.18)
    return jnp.clip(entries, -limit, limit).astype(kind)


def setup_inputs(seed: int = 0, part: int = 0) -> dict:
    seeds = jax.random.split(jax.random.key(seed), 14)
    own_keys = jax.random.split(jax.random.fold_in(seeds[13], part), 14)
    hidden_in = normal_values(own_keys[0], (STEPS, PARTICLES, D), 1.0, 6.0, ((1, 8),))
    queries = draw_queries(jax.random.fold_in(jax.random.fold_in(seeds[13], part), 71), part)
    new_keys = normal_values(own_keys[2], (STEPS, PARTICLES, KVH, HD), 1.0, 4.0, ((1, 8), (2, 2)))
    new_values = normal_values(own_keys[3], (STEPS, PARTICLES, KVH, HD), 2.0, 8.0, ((1, 8), (2, 2)))
    cache_keys = draw_cache_keys(jax.random.fold_in(jax.random.fold_in(seeds[13], part), 71), part)
    cache_values = normal_values(own_keys[5], (PARTICLES, KVH, CACHE, HD), 2.0, 8.0, ((0, 8), (1, 2)))
    route_ids_keys = jax.random.split(jax.random.fold_in(own_keys[6], 1), STEPS * PARTICLES // TOK_DEV)
    route_ids_turns = jax.random.permutation(jax.random.fold_in(own_keys[6], 3), STEPS * PARTICLES // TOK_DEV)
    route_ids = jax.vmap(lambda own, number: assign_block(jax.random.fold_in(own_keys[6], 2), own, number, TOK_DEV, EXPERTS, TOPK, CAP, 2))(route_ids_keys, route_ids_turns).reshape((STEPS, PARTICLES, TOPK))
    route_weights = jnp.clip(jnp.exp(math.log(1.0) - 2.3025851 * jax.random.uniform(own_keys[7], (STEPS, PARTICLES, TOPK), jnp.float32) ** steps_of(own_keys[7], (STEPS, PARTICLES, TOPK), ((1, 8),), -0.2, 0.2)), 0.1, 1.0)
    norm_gain = jnp.clip(1.0 + 0.15 * jax.random.normal(seeds[8], (D,), jnp.float32), 0.25, 1.75)
    gate_weight = normal_values(seeds[9], (EXPERTS, D, FF), D ** -0.5, 0.09375, ((0, 8), (2, 2)))
    up_weight = normal_values(seeds[10], (EXPERTS, D, FF), D ** -0.5, 0.09375, ((0, 8), (2, 2)))
    down_weight = normal_values(seeds[11], (EXPERTS, FF, D), FF ** -0.5, 0.21875, ((0, 8), (2, 2)))
    ancestor_counts = draw_ancestor_counts(jax.random.fold_in(jax.random.fold_in(seeds[13], part), 71), part)
    return dict(hidden_in=hidden_in, queries=queries, new_keys=new_keys, new_values=new_values, cache_keys=cache_keys, cache_values=cache_values, route_ids=route_ids, route_weights=route_weights, norm_gain=norm_gain, gate_weight=gate_weight, up_weight=up_weight, down_weight=down_weight, ancestor_counts=ancestor_counts)


epsilon = 1e-06
highest = lax.Precision.HIGHEST

def attention(queries, keys_all, values_all):
    group_size = QH // KVH
    length = CACHE + STEPS
    grouped = queries.astype(jnp.float32).reshape(STEPS, PARTICLES, KVH, group_size, HD)
    scores = jnp.einsum('sphgd,phld->sphgl', grouped, keys_all.astype(jnp.float32), precision=highest) / math.sqrt(HD)
    allowed = lax.broadcasted_iota(jnp.int32, (STEPS, length), 1) <= CACHE + lax.broadcasted_iota(jnp.int32, (STEPS, length), 0)
    scores = jnp.where(allowed[:, None, None, None, :], scores, -1e+30)
    exponent = jnp.exp(scores - lax.optimization_barrier(jnp.max(scores, axis=-1, keepdims=True)))
    probs = (exponent / lax.optimization_barrier(jnp.sum(exponent, axis=-1, keepdims=True))).astype(jnp.bfloat16)
    mixed = jnp.einsum('sphgl,phld->sphgd', probs.astype(jnp.float32), values_all.astype(jnp.float32), precision=highest)
    return mixed.astype(jnp.bfloat16).reshape(STEPS, PARTICLES, QH * HD)

def expert_rows(route_ids):
    blocks = PARTICLES // TOK_DEV
    pair_count = TOK_DEV * TOPK
    chosen = route_ids.reshape(STEPS, blocks, pair_count).astype(jnp.int32)
    expert_hits = (chosen[..., None] == jnp.arange(EXPERTS, dtype=jnp.int32)).astype(jnp.int32)
    position = lax.optimization_barrier(jnp.sum((jnp.cumsum(expert_hits, axis=2) - expert_hits) * expert_hits, axis=-1)).astype(jnp.int32)
    step_ids = lax.broadcasted_iota(jnp.int32, (STEPS, blocks, pair_count), 0)
    block_ids = lax.broadcasted_iota(jnp.int32, (STEPS, blocks, pair_count), 1)
    pair_ids = lax.broadcasted_iota(jnp.int32, (STEPS, blocks, pair_count), 2)
    slot_ids = ((chosen * STEPS + step_ids) * blocks + block_ids) * CAP + position
    token_ids = step_ids * PARTICLES + block_ids * TOK_DEV + pair_ids // TOPK
    return (slot_ids.reshape(-1).astype(jnp.int32), token_ids.reshape(-1).astype(jnp.int32))

def block_sum(split_rows, weight):
    blocks = weight.astype(jnp.float32).reshape(N_GROUP, D // N_GROUP, FF)
    terms = jnp.einsum('rgd,gdf->rgf', split_rows, blocks, precision=highest)
    return lax.optimization_barrier(jnp.sum(lax.optimization_barrier(terms.astype(jnp.bfloat16)).astype(jnp.float32), axis=1))

def mixture(normed, route_ids, route_weights, gate_weight, up_weight, down_weight):
    slot_ids, token_ids = expert_rows(route_ids)
    slot_total = EXPERTS * STEPS * (PARTICLES // TOK_DEV) * CAP
    holder = jnp.zeros((slot_total,), jnp.int32).at[slot_ids].set(token_ids + 1)
    flat_normed = normed.reshape(STEPS * PARTICLES, D)
    rows = flat_normed[jnp.maximum(holder - 1, 0)]
    rows = jnp.where((holder > 0)[:, None], rows, jnp.zeros((), jnp.bfloat16))
    rows = rows.reshape(EXPERTS, slot_total // EXPERTS, D)

    def one_expert(packed):
        block_rows, gate_matrix, up_matrix, down_matrix = packed
        split_rows = block_rows.astype(jnp.float32).reshape(-1, N_GROUP, D // N_GROUP)
        gate_sum = block_sum(split_rows, gate_matrix)
        up_sum = block_sum(split_rows, up_matrix)
        hidden = (jax.nn.silu(gate_sum) * up_sum).astype(jnp.bfloat16)
        return jnp.dot(hidden, down_matrix, preferred_element_type=jnp.float32).astype(jnp.bfloat16)
    outputs = lax.map(one_expert, (rows, gate_weight, up_weight, down_weight))
    outputs = outputs.reshape(slot_total, D)
    picked = outputs[slot_ids].astype(jnp.float32).reshape(STEPS, PARTICLES, TOPK, D)
    route_share = route_weights / lax.optimization_barrier(jnp.sum(route_weights, axis=-1, keepdims=True))
    return lax.optimization_barrier(jnp.sum(route_share[..., None] * picked, axis=2))

def reference(hidden_in, queries, new_keys, new_values, cache_keys, cache_values, route_ids, route_weights, norm_gain, gate_weight, up_weight, down_weight, ancestor_counts):
    keys_all = jnp.concatenate([cache_keys, jnp.transpose(new_keys, (1, 2, 0, 3))], axis=2)
    values_all = jnp.concatenate([cache_values, jnp.transpose(new_values, (1, 2, 0, 3))], axis=2)
    attended = attention(queries, keys_all, values_all)
    residual = hidden_in.astype(jnp.float32) + attended.astype(jnp.float32)
    normed = (residual * lax.rsqrt(lax.optimization_barrier(jnp.mean(residual * residual, axis=-1, keepdims=True)) + epsilon) * norm_gain).astype(jnp.bfloat16)
    expert_mix = mixture(normed, route_ids, route_weights, gate_weight, up_weight, down_weight)
    layer_out = (residual + expert_mix).astype(jnp.bfloat16)
    running = jnp.cumsum(ancestor_counts)
    indices = jnp.arange(PARTICLES, dtype=jnp.int32)
    ancestor = lax.optimization_barrier(jnp.sum((running[None, :] <= indices[:, None]).astype(jnp.int32), axis=1))
    return (layer_out, keys_all[ancestor], values_all[ancestor])
```

```python
import math

import jax
import jax.numpy as jnp
from jax import lax
from jax.sharding import PartitionSpec as P

REACH = 2


epsilon = 1e-06
highest = lax.Precision.HIGHEST


def padded(cells, sides, width):
    for axis, dim in sides:
        count = lax.axis_size(axis)
        ends = count - 1
        head = lax.slice_in_dim(cells, 0, width, axis=dim)
        tail = lax.slice_in_dim(cells, cells.shape[dim] - width, cells.shape[dim], axis=dim)
        cells = jnp.concatenate(
            [
                lax.ppermute(tail, axis, [(i, (i + 1) % count) for i in range(ends)]),
                cells,
                lax.ppermute(head, axis, [((i + 1) % count, i) for i in range(ends)]),
            ],
            axis=dim,
        )
    return cells


def grouped_shards(
    hidden_in,
    queries,
    new_keys,
    new_values,
    cache_keys,
    cache_values,
    route_ids,
    route_weights,
    norm_gain,
    gate_weight,
    up_weight,
    down_weight,
    ancestor_counts,
):
    step_count, token_count, query_heads, head_width = queries.shape
    key_heads = cache_keys.shape[1]
    cached = cache_keys.shape[2]
    group_size = query_heads // key_heads
    cache_pair = jnp.stack([cache_keys, cache_values])
    fresh_pair = jnp.transpose(jnp.stack([new_keys, new_values]), (0, 2, 3, 1, 4))
    both_kv = jnp.concatenate([cache_pair, fresh_pair], axis=3)
    length = both_kv.shape[3]
    grouped = queries.reshape(step_count, token_count, key_heads, group_size, head_width)
    scores = jnp.einsum(
        "sphgd,phld->sphgl", grouped, both_kv[0], preferred_element_type=jnp.float32
    ) / math.sqrt(head_width)
    allowed = lax.broadcasted_iota(
        jnp.int32, (step_count, length), 1
    ) <= cached + lax.broadcasted_iota(jnp.int32, (step_count, length), 0)
    scores = jnp.where(allowed[:, None, None, None, :], scores, -1e30)
    exponent = jnp.exp(scores - jnp.max(scores, axis=-1, keepdims=True))
    attn_weights = (exponent / jnp.sum(exponent, axis=-1, keepdims=True)).astype(jnp.bfloat16)
    attended = jnp.einsum(
        "sphgl,phld->sphgd", attn_weights, both_kv[1], preferred_element_type=jnp.float32
    )
    attended = attended.astype(jnp.bfloat16).reshape(
        step_count, token_count, query_heads * head_width
    )
    attended = lax.all_gather(attended, "tensor", axis=2, tiled=True)
    expert_count = lax.axis_size("expert")
    group_count = lax.axis_size("group")
    tensor_count = lax.axis_size("tensor")
    tensor_index = lax.axis_index("tensor")
    expert_local = gate_weight.shape[0]
    experts_all = expert_local * expert_count
    chosen_count = route_ids.shape[2]
    model_width = hidden_in.shape[2]
    column_width = down_weight.shape[2]
    capacity = min(token_count, max(2, 2 * token_count * chosen_count // experts_all))
    pair_count = token_count * chosen_count
    expert_iota = jnp.arange(experts_all, dtype=jnp.int32)
    slot_iota = jnp.arange(capacity, dtype=jnp.int32)
    token_owner = (
        (jnp.arange(pair_count) // chosen_count)[:, None] == jnp.arange(token_count)[None, :]
    ).astype(jnp.float32)
    halves = []
    for step_index in range(step_count):
        residual = hidden_in[step_index].astype(jnp.float32) + attended[step_index].astype(
            jnp.float32
        )
        normed = (
            residual
            * lax.rsqrt(jnp.mean(residual * residual, axis=-1, keepdims=True) + epsilon)
            * norm_gain
        ).astype(jnp.bfloat16)
        chosen = route_ids[step_index].reshape(pair_count)
        route_share = route_weights[step_index] / jnp.sum(
            route_weights[step_index], axis=-1, keepdims=True
        )
        expert_hits = (chosen[:, None] == expert_iota[None, :]).astype(jnp.int32)
        position = jnp.sum((jnp.cumsum(expert_hits, axis=0) - expert_hits) * expert_hits, axis=1)
        slotted = (
            expert_hits[:, :, None]
            * (position[:, None, None] == slot_iota[None, None, :]).astype(jnp.int32)
        ).astype(jnp.float32)
        dispatch = jnp.einsum("rec,rt->ect", slotted, token_owner, precision=highest)
        dispatch = dispatch.reshape(expert_count, expert_local, capacity, token_count).astype(
            jnp.bfloat16
        )
        combine = jnp.einsum(
            "rec,rt,r->tec",
            slotted,
            token_owner,
            route_share.reshape(pair_count),
            precision=highest,
        )
        combine = combine.reshape(token_count, expert_count, expert_local, capacity)
        feature_blocks = normed.reshape(token_count, group_count, model_width // group_count)
        outgoing = jnp.einsum(
            "aict,tgd->agicd", dispatch, feature_blocks, preferred_element_type=jnp.float32
        ).astype(jnp.bfloat16)
        flattened = outgoing.reshape(
            expert_count * group_count, expert_local, capacity, model_width // group_count
        )
        received = lax.all_to_all(
            flattened, ("expert", "group"), split_axis=0, concat_axis=0, tiled=True
        )
        gate_part = jnp.einsum(
            "seki,eif->sekf", received, gate_weight, preferred_element_type=jnp.float32
        ).astype(jnp.bfloat16)
        up_part = jnp.einsum(
            "seki,eif->sekf", received, up_weight, preferred_element_type=jnp.float32
        ).astype(jnp.bfloat16)
        gate_sum = lax.psum(gate_part, "group").astype(jnp.float32)
        up_sum = lax.psum(up_part, "group").astype(jnp.float32)
        hidden = (jax.nn.silu(gate_sum) * up_sum).astype(jnp.bfloat16)
        hidden = lax.all_gather(hidden, "tensor", axis=3, tiled=True)
        answered = jnp.einsum(
            "sekf,efo->seko", hidden, down_weight, preferred_element_type=jnp.float32
        ).astype(jnp.bfloat16)
        returned = lax.all_to_all(
            answered, ("expert", "group"), split_axis=0, concat_axis=0, tiled=True
        )
        returned = returned.reshape(
            expert_count, group_count, expert_local, capacity, column_width
        ).astype(jnp.float32)
        expert_mix = jnp.einsum("taic,agicd->tgd", combine, returned, precision=highest)
        own_columns = lax.dynamic_index_in_dim(
            residual.reshape(token_count, group_count, tensor_count, column_width),
            tensor_index,
            2,
            keepdims=False,
        )
        halves.append((own_columns + expert_mix).astype(jnp.bfloat16))
    stacked = jnp.stack(halves)
    layer_out = lax.all_gather(stacked, "tensor", axis=3, tiled=True).reshape(
        step_count, token_count, model_width
    )
    every_count = lax.all_gather(ancestor_counts, ("expert", "group"), axis=0, tiled=True)
    running = jnp.cumsum(every_count)
    first_index = lax.axis_index(("expert", "group")) * token_count
    own_index = first_index + jnp.arange(token_count, dtype=jnp.int32)
    ancestor = jnp.sum((running[None, :] <= own_index[:, None]).astype(jnp.int32), axis=1)
    widened = padded(both_kv, ((("expert", "group"), 1),), REACH)
    window_index = first_index - REACH + jnp.arange(token_count + 2 * REACH, dtype=jnp.int32)
    selector = (ancestor[:, None] == window_index[None, :]).astype(jnp.bfloat16)
    resampled = jnp.einsum(
        "tw,kwhld->kthld", selector, widened, preferred_element_type=jnp.float32
    ).astype(jnp.bfloat16)
    return (layer_out, resampled[0], resampled[1])


def one_group_shards(
    hidden_in,
    queries,
    new_keys,
    new_values,
    cache_keys,
    cache_values,
    route_ids,
    route_weights,
    norm_gain,
    gate_weight,
    up_weight,
    down_weight,
    ancestor_counts,
):
    step_count, token_count, query_heads, head_width = queries.shape
    key_heads = cache_keys.shape[1]
    cached = cache_keys.shape[2]
    group_size = query_heads // key_heads
    rows = step_count * token_count
    model_width = hidden_in.shape[2]
    expert_count = lax.axis_size("expert")
    expert_index = lax.axis_index("expert")
    expert_local = gate_weight.shape[0]
    experts_all = expert_local * expert_count
    column_width = down_weight.shape[2]
    tensor_index = lax.axis_index("tensor")
    cache_pair = jnp.stack([cache_keys, cache_values])
    fresh_pair = jnp.transpose(jnp.stack([new_keys, new_values]), (0, 2, 3, 1, 4))
    both_kv = jnp.concatenate([cache_pair, fresh_pair], axis=3)
    length = both_kv.shape[3]
    grouped = queries.reshape(step_count, token_count, key_heads, group_size, head_width)
    scores = jnp.einsum(
        "sphgd,phld->sphgl", grouped, both_kv[0], preferred_element_type=jnp.float32
    ) / math.sqrt(head_width)
    allowed = lax.broadcasted_iota(
        jnp.int32, (step_count, length), 1
    ) <= cached + lax.broadcasted_iota(jnp.int32, (step_count, length), 0)
    scores = jnp.where(allowed[:, None, None, None, :], scores, -1e30)
    exponent = jnp.exp(scores - jnp.max(scores, axis=-1, keepdims=True))
    attn_weights = (exponent / jnp.sum(exponent, axis=-1, keepdims=True)).astype(jnp.bfloat16)
    attended = jnp.einsum(
        "sphgl,phld->sphgd", attn_weights, both_kv[1], preferred_element_type=jnp.float32
    )
    attended = attended.astype(jnp.bfloat16).reshape(rows, query_heads * head_width)
    attended = lax.all_gather(attended, "tensor", axis=1, tiled=True)
    residual = hidden_in.reshape(rows, model_width).astype(jnp.float32) + attended.astype(
        jnp.float32
    )
    normed = (
        residual
        * lax.rsqrt(jnp.mean(residual * residual, axis=-1, keepdims=True) + epsilon)
        * norm_gain
    ).astype(jnp.bfloat16)
    share = route_weights / jnp.sum(route_weights, axis=-1, keepdims=True)
    hits = route_ids[..., None] == jnp.arange(experts_all, dtype=jnp.int32)
    mix = jnp.sum(jnp.where(hits, share[..., None], 0.0), axis=2).reshape(rows, experts_all)
    counts = jnp.broadcast_to(ancestor_counts.astype(jnp.float32)[None, :], (rows, token_count))
    table = jnp.concatenate([mix, counts], axis=1)
    spare = -table.shape[1] % 128
    table = jnp.pad(table, ((0, 0), (0, spare)))
    table = lax.all_gather(table, "expert", axis=0, tiled=True)
    tokens = lax.all_gather(normed, "expert", axis=0, tiled=True)
    gate = jnp.einsum("ri,eif->erf", tokens, gate_weight, preferred_element_type=jnp.float32)
    up = jnp.einsum("ri,eif->erf", tokens, up_weight, preferred_element_type=jnp.float32)
    gate = gate.astype(jnp.bfloat16).astype(jnp.float32)
    up = up.astype(jnp.bfloat16).astype(jnp.float32)
    hidden = (jax.nn.silu(gate) * up).astype(jnp.bfloat16)
    hidden = lax.all_gather(hidden, "tensor", axis=2, tiled=True)
    answered = jnp.einsum(
        "erf,efo->ero", hidden, down_weight, preferred_element_type=jnp.float32
    )
    own_mix = lax.dynamic_slice_in_dim(table, expert_index * expert_local, expert_local, axis=1)
    partial = jnp.sum(answered * own_mix.T[:, :, None], axis=0).astype(jnp.bfloat16)
    returned = lax.all_to_all(
        partial.reshape(expert_count, rows, column_width), "expert", 0, 0, tiled=True
    )
    expert_mix = jnp.sum(returned.astype(jnp.float32), axis=0)
    own_columns = lax.dynamic_slice_in_dim(
        residual, tensor_index * column_width, column_width, axis=1
    )
    half = (own_columns + expert_mix).astype(jnp.bfloat16)
    layer_out = lax.all_gather(half, "tensor", axis=1, tiled=True).reshape(
        step_count, token_count, model_width
    )
    every_count = table.reshape(expert_count, rows, -1)[
        :, 0, experts_all : experts_all + token_count
    ].reshape(-1)
    running = jnp.cumsum(every_count.astype(jnp.int32))
    first_index = expert_index * token_count
    own_index = first_index + jnp.arange(token_count, dtype=jnp.int32)
    ancestor = jnp.sum((running[None, :] <= own_index[:, None]).astype(jnp.int32), axis=1)
    widened = padded(both_kv, ((("expert", "group"), 1),), REACH)
    window_index = first_index - REACH + jnp.arange(token_count + 2 * REACH, dtype=jnp.int32)
    selector = (ancestor[:, None] == window_index[None, :]).astype(jnp.bfloat16)
    resampled = jnp.einsum(
        "tw,kwhld->kthld", selector, widened, preferred_element_type=jnp.float32
    ).astype(jnp.bfloat16)
    return (layer_out, resampled[0], resampled[1])


def solution(mesh):
    shards = one_group_shards if mesh.shape["group"] == 1 else grouped_shards
    in_specs = (
        P(None, ("parts", "expert", "group"), None),
        P(None, ("parts", "expert", "group"), "tensor", None),
        P(None, ("parts", "expert", "group"), "tensor", None),
        P(None, ("parts", "expert", "group"), "tensor", None),
        P(("parts", "expert", "group"), "tensor", None, None),
        P(("parts", "expert", "group"), "tensor", None, None),
        P(None, ("parts", "expert", "group"), None),
        P(None, ("parts", "expert", "group"), None),
        P(),
        P("expert", "group", "tensor"),
        P("expert", "group", "tensor"),
        P("expert", None, ("group", "tensor")),
        P(("parts", "expert", "group")),
    )
    out_specs = (
        P(None, ("parts", "expert", "group"), None),
        P(("parts", "expert", "group"), "tensor", None, None),
        P(("parts", "expert", "group"), "tensor", None, None),
    )
    return jax.shard_map(shards, mesh=mesh, in_specs=in_specs, out_specs=out_specs, check_vma=False)
```

```python
import functools
import math

import jax
import jax.numpy as jnp
from jax import lax
from jax.experimental import pallas as pl
from jax.experimental.pallas import tpu as pltpu
from jax.sharding import PartitionSpec as P

REACH = 2


epsilon = 1e-06
highest = lax.Precision.HIGHEST


def padded(cells, sides, width):
    for axis, dim in sides:
        count = lax.axis_size(axis)
        ends = count - 1
        head = lax.slice_in_dim(cells, 0, width, axis=dim)
        tail = lax.slice_in_dim(cells, cells.shape[dim] - width, cells.shape[dim], axis=dim)
        cells = jnp.concatenate(
            [
                lax.ppermute(tail, axis, [(i, (i + 1) % count) for i in range(ends)]),
                cells,
                lax.ppermute(head, axis, [((i + 1) % count, i) for i in range(ends)]),
            ],
            axis=dim,
        )
    return cells


def grouped_shards(
    hidden_in,
    queries,
    new_keys,
    new_values,
    cache_keys,
    cache_values,
    route_ids,
    route_weights,
    norm_gain,
    gate_weight,
    up_weight,
    down_weight,
    ancestor_counts,
):
    step_count, token_count, query_heads, head_width = queries.shape
    key_heads = cache_keys.shape[1]
    cached = cache_keys.shape[2]
    group_size = query_heads // key_heads
    cache_pair = jnp.stack([cache_keys, cache_values])
    fresh_pair = jnp.transpose(jnp.stack([new_keys, new_values]), (0, 2, 3, 1, 4))
    both_kv = jnp.concatenate([cache_pair, fresh_pair], axis=3)
    length = both_kv.shape[3]
    grouped = queries.reshape(step_count, token_count, key_heads, group_size, head_width)
    scores = jnp.einsum(
        "sphgd,phld->sphgl", grouped, both_kv[0], preferred_element_type=jnp.float32
    ) / math.sqrt(head_width)
    allowed = lax.broadcasted_iota(
        jnp.int32, (step_count, length), 1
    ) <= cached + lax.broadcasted_iota(jnp.int32, (step_count, length), 0)
    scores = jnp.where(allowed[:, None, None, None, :], scores, -1e30)
    exponent = jnp.exp(scores - jnp.max(scores, axis=-1, keepdims=True))
    attn_weights = (exponent / jnp.sum(exponent, axis=-1, keepdims=True)).astype(jnp.bfloat16)
    attended = jnp.einsum(
        "sphgl,phld->sphgd", attn_weights, both_kv[1], preferred_element_type=jnp.float32
    )
    attended = attended.astype(jnp.bfloat16).reshape(
        step_count, token_count, query_heads * head_width
    )
    attended = lax.all_gather(attended, "tensor", axis=2, tiled=True)
    expert_count = lax.axis_size("expert")
    group_count = lax.axis_size("group")
    tensor_count = lax.axis_size("tensor")
    tensor_index = lax.axis_index("tensor")
    expert_local = gate_weight.shape[0]
    experts_all = expert_local * expert_count
    chosen_count = route_ids.shape[2]
    model_width = hidden_in.shape[2]
    column_width = down_weight.shape[2]
    capacity = min(token_count, max(2, 2 * token_count * chosen_count // experts_all))
    pair_count = token_count * chosen_count
    expert_iota = jnp.arange(experts_all, dtype=jnp.int32)
    slot_iota = jnp.arange(capacity, dtype=jnp.int32)
    token_owner = (
        (jnp.arange(pair_count) // chosen_count)[:, None] == jnp.arange(token_count)[None, :]
    ).astype(jnp.float32)
    halves = []
    for step_index in range(step_count):
        residual = hidden_in[step_index].astype(jnp.float32) + attended[step_index].astype(
            jnp.float32
        )
        normed = (
            residual
            * lax.rsqrt(jnp.mean(residual * residual, axis=-1, keepdims=True) + epsilon)
            * norm_gain
        ).astype(jnp.bfloat16)
        chosen = route_ids[step_index].reshape(pair_count)
        route_share = route_weights[step_index] / jnp.sum(
            route_weights[step_index], axis=-1, keepdims=True
        )
        expert_hits = (chosen[:, None] == expert_iota[None, :]).astype(jnp.int32)
        position = jnp.sum((jnp.cumsum(expert_hits, axis=0) - expert_hits) * expert_hits, axis=1)
        slotted = (
            expert_hits[:, :, None]
            * (position[:, None, None] == slot_iota[None, None, :]).astype(jnp.int32)
        ).astype(jnp.float32)
        dispatch = jnp.einsum("rec,rt->ect", slotted, token_owner, precision=highest)
        dispatch = dispatch.reshape(expert_count, expert_local, capacity, token_count).astype(
            jnp.bfloat16
        )
        combine = jnp.einsum(
            "rec,rt,r->tec",
            slotted,
            token_owner,
            route_share.reshape(pair_count),
            precision=highest,
        )
        combine = combine.reshape(token_count, expert_count, expert_local, capacity)
        feature_blocks = normed.reshape(token_count, group_count, model_width // group_count)
        outgoing = jnp.einsum(
            "aict,tgd->agicd", dispatch, feature_blocks, preferred_element_type=jnp.float32
        ).astype(jnp.bfloat16)
        flattened = outgoing.reshape(
            expert_count * group_count, expert_local, capacity, model_width // group_count
        )
        received = lax.all_to_all(
            flattened, ("expert", "group"), split_axis=0, concat_axis=0, tiled=True
        )
        gate_part = jnp.einsum(
            "seki,eif->sekf", received, gate_weight, preferred_element_type=jnp.float32
        ).astype(jnp.bfloat16)
        up_part = jnp.einsum(
            "seki,eif->sekf", received, up_weight, preferred_element_type=jnp.float32
        ).astype(jnp.bfloat16)
        gate_sum = lax.psum(gate_part, "group").astype(jnp.float32)
        up_sum = lax.psum(up_part, "group").astype(jnp.float32)
        hidden = (jax.nn.silu(gate_sum) * up_sum).astype(jnp.bfloat16)
        hidden = lax.all_gather(hidden, "tensor", axis=3, tiled=True)
        answered = jnp.einsum(
            "sekf,efo->seko", hidden, down_weight, preferred_element_type=jnp.float32
        ).astype(jnp.bfloat16)
        returned = lax.all_to_all(
            answered, ("expert", "group"), split_axis=0, concat_axis=0, tiled=True
        )
        returned = returned.reshape(
            expert_count, group_count, expert_local, capacity, column_width
        ).astype(jnp.float32)
        expert_mix = jnp.einsum("taic,agicd->tgd", combine, returned, precision=highest)
        own_columns = lax.dynamic_index_in_dim(
            residual.reshape(token_count, group_count, tensor_count, column_width),
            tensor_index,
            2,
            keepdims=False,
        )
        halves.append((own_columns + expert_mix).astype(jnp.bfloat16))
    stacked = jnp.stack(halves)
    layer_out = lax.all_gather(stacked, "tensor", axis=3, tiled=True).reshape(
        step_count, token_count, model_width
    )
    every_count = lax.all_gather(ancestor_counts, ("expert", "group"), axis=0, tiled=True)
    running = jnp.cumsum(every_count)
    first_index = lax.axis_index(("expert", "group")) * token_count
    own_index = first_index + jnp.arange(token_count, dtype=jnp.int32)
    ancestor = jnp.sum((running[None, :] <= own_index[:, None]).astype(jnp.int32), axis=1)
    widened = padded(both_kv, ((("expert", "group"), 1),), REACH)
    window_index = first_index - REACH + jnp.arange(token_count + 2 * REACH, dtype=jnp.int32)
    selector = (ancestor[:, None] == window_index[None, :]).astype(jnp.bfloat16)
    resampled = jnp.einsum(
        "tw,kwhld->kthld", selector, widened, preferred_element_type=jnp.float32
    ).astype(jnp.bfloat16)
    return (layer_out, resampled[0], resampled[1])


MESH = pl.DeviceIdType.MESH
CHUNKS = 2


def step_kernel(
    dims,
    hidden_ref,
    query_ref,
    fresh_ref,
    keys_ref,
    values_ref,
    table_ref,
    gain_ref,
    gate_hbm,
    up_hbm,
    down_hbm,
    out_ref,
    keys_out,
    values_out,
    both,
    heads,
    square,
    tokens,
    tables,
    gate_w,
    up_w,
    down_w,
    hidden,
    parts,
    returned,
    halves,
    halo,
    weight_sem,
    square_sem,
    token_send,
    token_recv,
    pass_send,
    pass_recv,
    table_send,
    table_recv,
    hidden_sem,
    part_send,
    part_recv,
    half_sem,
    halo_sem,
):
    steps, toks, key_heads, cached, total, half = dims
    rows = steps * toks
    count = lax.axis_size("expert")
    me = lax.axis_index("expert")
    side = lax.axis_index("tensor")
    other = 1 - side
    peers = [lax.rem(me + k, count) for k in range(1, count)]
    padded_rows = tokens.shape[2]
    experts = gate_w.shape[0]
    query_heads = query_ref.shape[2]
    head_width = query_ref.shape[3]
    bf16, f32 = jnp.bfloat16, jnp.float32

    barrier = pltpu.get_barrier_semaphore()
    for peer in peers:
        pl.semaphore_signal(barrier, inc=1, device_id={"expert": peer}, device_id_type=MESH)
    pl.semaphore_signal(barrier, inc=1, device_id={"tensor": other}, device_id_type=MESH)

    loads = [
        pltpu.make_async_copy(gate_hbm, gate_w, weight_sem.at[0]),
        pltpu.make_async_copy(up_hbm, up_w, weight_sem.at[1]),
        pltpu.make_async_copy(down_hbm, down_w, weight_sem.at[2]),
    ]
    for load in loads:
        load.start()

    tables[me] = table_ref[...]
    both[0, :, :, 0:cached, :] = keys_ref[...]
    both[1, :, :, 0:cached, :] = values_ref[...]
    both[:, :, :, cached:, :] = fresh_ref[...]
    length = both.shape[3]

    step_rows = steps * query_heads
    row = lax.broadcasted_iota(jnp.int32, (step_rows, length), 0)
    lane = lax.broadcasted_iota(jnp.int32, (step_rows, length), 1)
    allowed = lane <= cached + row // query_heads
    head_of = (row % query_heads) // (query_heads // key_heads)
    head_of_out = head_of[:, 0:head_width]
    for p in range(toks):
        q = jnp.concatenate([query_ref[s, p] for s in range(steps)], axis=0)
        scores = jnp.zeros((step_rows, length), f32)
        for h in range(key_heads):
            one = lax.dot_general(
                q, both[0, p, h], (((1,), (1,)), ((), ())), preferred_element_type=f32
            )
            scores = jnp.where(head_of == h, one, scores)
        scores = jnp.where(allowed, scores / math.sqrt(head_width), -1e30)
        exponent = jnp.exp(scores - jnp.max(scores, axis=-1, keepdims=True))
        probs = (exponent / jnp.sum(exponent, axis=-1, keepdims=True)).astype(bf16)
        mixed = jnp.zeros((step_rows, head_width), f32)
        for h in range(key_heads):
            one = jnp.dot(probs, both[1, p, h], preferred_element_type=f32)
            mixed = jnp.where(head_of_out == h, one, mixed)
        mixed = mixed.astype(bf16).astype(f32)
        for s in range(steps):
            at = (s * toks + p) * query_heads
            heads[at : at + query_heads, :] = mixed[s * query_heads : (s + 1) * query_heads]
    attended = jnp.concatenate(
        [heads[pl.ds(h, rows, stride=query_heads), :] for h in range(query_heads)], axis=1
    )
    own_lanes = pl.ds(pl.multiple_of(side * half, half), half)
    incoming = jnp.concatenate(
        [hidden_ref[s, :, own_lanes].astype(f32) for s in range(steps)], axis=0
    )
    residual = incoming + attended
    squares = jnp.sum(residual * residual, axis=-1, keepdims=True)
    fill = jnp.zeros((padded_rows - rows, 128), f32)
    square[0] = jnp.concatenate([jnp.broadcast_to(squares, (rows, 128)), fill], axis=0)

    pl.semaphore_wait(barrier, count)

    square_copy = pltpu.make_async_remote_copy(
        src_ref=square.at[0],
        dst_ref=square.at[1],
        send_sem=square_sem.at[0],
        recv_sem=square_sem.at[1],
        device_id={"tensor": other},
        device_id_type=MESH,
    )
    square_copy.start()

    def table_copy(k):
        return pltpu.make_async_remote_copy(
            src_ref=tables.at[me],
            dst_ref=tables.at[me],
            send_sem=table_send.at[k],
            recv_sem=table_recv.at[me],
            device_id={"expert": peers[k]},
            device_id_type=MESH,
        )

    for k in range(count - 1):
        table_copy(k).start()

    square_copy.wait()
    mean = (square[0, 0:rows, 0:1] + square[1, 0:rows, 0:1]) / (2 * half)
    normed = residual * lax.rsqrt(mean + epsilon) * gain_ref[:, own_lanes]
    normed = jnp.concatenate([normed, jnp.zeros((padded_rows - rows, half), f32)], axis=0)
    tokens[side, me] = normed.astype(bf16)

    def token_copy(k):
        return pltpu.make_async_remote_copy(
            src_ref=tokens.at[side, me],
            dst_ref=tokens.at[side, me],
            send_sem=token_send.at[k],
            recv_sem=token_recv.at[me],
            device_id={"expert": peers[k]},
            device_id_type=MESH,
        )

    def pass_copy(d):
        return pltpu.make_async_remote_copy(
            src_ref=tokens.at[side, d],
            dst_ref=tokens.at[side, d],
            send_sem=pass_send.at[d],
            recv_sem=pass_recv.at[d],
            device_id={"tensor": other},
            device_id_type=MESH,
        )

    def arrival(buffer, sem, k):
        d = peers[k]
        return pltpu.make_async_remote_copy(
            src_ref=buffer.at[d],
            dst_ref=buffer.at[d],
            send_sem=sem.at[d],
            recv_sem=sem.at[d],
            device_id={"expert": d},
            device_id_type=MESH,
        )

    for k in range(count - 1):
        token_copy(k).start()
    pass_copy(me).start()
    order = list(range(count - 1))
    for k in order:
        arrival(tokens.at[side], token_recv, k).wait_recv()
        pass_copy(peers[k]).start()

    def halo_copy(way):
        first = toks - REACH if way == 0 else 0
        return pltpu.make_async_remote_copy(
            src_ref=both.at[:, first : first + REACH],
            dst_ref=halo.at[way],
            send_sem=halo_sem.at[0, way],
            recv_sem=halo_sem.at[1, way],
            device_id={"expert": lax.rem(me + (1 if way == 0 else count - 1), count)},
            device_id_type=MESH,
        )

    @pl.when(me < count - 1)
    def _():
        halo_copy(0).start()

    @pl.when(me > 0)
    def _():
        halo_copy(1).start()

    loads[0].wait()
    loads[1].wait()
    all_rows = count * padded_rows
    gates, ups = [], []
    own_depth = pl.ds(pl.multiple_of(side * half, half), half)
    other_depth = pl.ds(pl.multiple_of(other * half, half), half)
    held = tokens[side].reshape(all_rows, half)
    for e in range(experts):
        gates.append(jnp.dot(held, gate_w[e, own_depth, :], preferred_element_type=f32))
        ups.append(jnp.dot(held, up_w[e, own_depth, :], preferred_element_type=f32))

    def pass_arrival(d):
        return pltpu.make_async_remote_copy(
            src_ref=tokens.at[other, d],
            dst_ref=tokens.at[other, d],
            send_sem=pass_send.at[d],
            recv_sem=pass_recv.at[d],
            device_id={"tensor": other},
            device_id_type=MESH,
        )

    pass_arrival(me).wait_recv()
    for k in order:
        pass_arrival(peers[k]).wait_recv()
    held = tokens[other].reshape(all_rows, half)

    def hidden_copy(e):
        return pltpu.make_async_remote_copy(
            src_ref=hidden.at[side, e],
            dst_ref=hidden.at[side, e],
            send_sem=hidden_sem.at[0, e],
            recv_sem=hidden_sem.at[1, e],
            device_id={"tensor": other},
            device_id_type=MESH,
        )

    def hidden_arrival(e):
        return pltpu.make_async_remote_copy(
            src_ref=hidden.at[other, e],
            dst_ref=hidden.at[other, e],
            send_sem=hidden_sem.at[0, e],
            recv_sem=hidden_sem.at[1, e],
            device_id={"tensor": other},
            device_id_type=MESH,
        )

    for e in range(experts):
        gate = gates[e] + jnp.dot(held, gate_w[e, other_depth, :], preferred_element_type=f32)
        up = ups[e] + jnp.dot(held, up_w[e, other_depth, :], preferred_element_type=f32)
        gate = gate.astype(bf16).astype(f32)
        up = up.astype(bf16).astype(f32)
        hidden[side, e] = (gate / (1.0 + jnp.exp(-gate)) * up).astype(bf16)
        hidden_copy(e).start()

    for k in order:
        arrival(tables, table_recv, k).wait_recv()
    everything = tables[...]
    mix = everything[:, 0:padded_rows, :].reshape(all_rows, 128)
    mix_lane = lax.broadcasted_iota(jnp.int32, (all_rows, 128), 1)
    shares = [
        jnp.sum(jnp.where(mix_lane == me * experts + e, mix, 0.0), axis=1, keepdims=True)
        for e in range(experts)
    ]

    loads[2].wait()
    activations = []
    for e in range(experts):
        hidden_arrival(e).wait_recv()
        activations.append(jnp.concatenate([hidden[0, e], hidden[1, e]], axis=1))

    def part_copy(c, k):
        return pltpu.make_async_remote_copy(
            src_ref=parts.at[c, peers[k]],
            dst_ref=returned.at[c, me],
            send_sem=part_send.at[c, k],
            recv_sem=part_recv.at[c, me],
            device_id={"expert": peers[k]},
            device_id_type=MESH,
        )

    width = half // CHUNKS
    for c in range(CHUNKS):
        mixture = jnp.zeros((all_rows, width), f32)
        for e in range(experts):
            answered = jnp.dot(
                activations[e],
                down_w[e, :, c * width : (c + 1) * width],
                preferred_element_type=f32,
            )
            mixture = mixture + shares[e] * answered
        parts[c] = mixture.astype(bf16).reshape(count, padded_rows, width)
        for k in order:
            part_copy(c, k).start()

    @pl.when(me > 0)
    def _():
        halo_copy(0).wait_recv()

    @pl.when(me == 0)
    def _():
        halo[0] = jnp.zeros(halo.shape[1:], bf16)

    @pl.when(me < count - 1)
    def _():
        halo_copy(1).wait_recv()

    @pl.when(me == count - 1)
    def _():
        halo[1] = jnp.zeros(halo.shape[1:], bf16)

    counts = jnp.sum(everything[:, padded_rows:, :], axis=0)
    below = lax.broadcasted_iota(jnp.int32, (128, 128), 0)
    above = lax.broadcasted_iota(jnp.int32, (128, 128), 1)
    running = jnp.dot(
        counts, jnp.where(below <= above, 1.0, 0.0).astype(f32), preferred_element_type=f32
    )
    running = jnp.broadcast_to(running[0:1], (8, 128))
    place = me * toks + lax.broadcasted_iota(jnp.int32, (8, 128), 0)
    which = lax.broadcasted_iota(jnp.int32, (8, 128), 1)
    passed = jnp.where((running <= place.astype(f32)) & (which < total), 1.0, 0.0)
    ancestor = jnp.sum(passed, axis=1, keepdims=True)
    relative = ancestor - (me * toks - REACH).astype(f32)
    for t in range(toks):
        at = jnp.broadcast_to(relative[t : t + 1, :], (length, head_width))
        picks = [
            (w, jnp.where(at == float(w), 1.0, 0.0)) for w in range(t, t + 2 * REACH + 1)
        ]
        for kv, target in ((0, keys_out), (1, values_out)):
            for h in range(key_heads):
                chosen = jnp.zeros((length, head_width), f32)
                for w, pick in picks:
                    if w < REACH:
                        source = halo[0, kv, w, h]
                    elif w < REACH + toks:
                        source = both[kv, w - REACH, h]
                    else:
                        source = halo[1, kv, w - REACH - toks, h]
                    chosen = chosen + pick * source.astype(f32)
                target[t, h] = chosen.astype(bf16)[0 : cached + steps]

    sums = []
    for c in range(CHUNKS):
        for k in order:
            arrival(returned.at[c], part_recv.at[c], k).wait_recv()
        summed = parts[c, me].astype(f32)
        for k in order:
            summed = summed + returned[c, peers[k]].astype(f32)
        sums.append(summed)
    layer = residual + jnp.concatenate(sums, axis=1)[0:rows]
    layer = jnp.concatenate([layer, jnp.zeros((padded_rows - rows, half), f32)], axis=0)
    halves[side] = layer.astype(bf16)

    def half_copy(which_half):
        return pltpu.make_async_remote_copy(
            src_ref=halves.at[which_half],
            dst_ref=halves.at[which_half],
            send_sem=half_sem.at[0],
            recv_sem=half_sem.at[1],
            device_id={"tensor": other},
            device_id_type=MESH,
        )

    half_copy(side).start()
    for k in order:
        table_copy(k).wait_send()
        token_copy(k).wait_send()
        pass_copy(peers[k]).wait_send()
        for c in range(CHUNKS):
            part_copy(c, k).wait_send()
    pass_copy(me).wait_send()
    for e in range(experts):
        hidden_copy(e).wait_send()

    @pl.when(me < count - 1)
    def _():
        halo_copy(0).wait_send()

    @pl.when(me > 0)
    def _():
        halo_copy(1).wait_send()

    half_copy(other).wait_recv()
    whole = jnp.concatenate([halves[0], halves[1]], axis=1).astype(f32)
    for s in range(steps):
        out_ref[s] = whole[s * toks : (s + 1) * toks].astype(bf16)
    half_copy(side).wait_send()


def one_group_shards(
    hidden_in,
    queries,
    new_keys,
    new_values,
    cache_keys,
    cache_values,
    route_ids,
    route_weights,
    norm_gain,
    gate_weight,
    up_weight,
    down_weight,
    ancestor_counts,
):
    steps, toks, query_heads, head_width = queries.shape
    key_heads, cached = cache_keys.shape[1:3]
    rows = steps * toks
    padded_rows = -(-rows // 16) * 16
    length = -(-(cached + steps) // 16) * 16
    model_width = hidden_in.shape[2]
    half = down_weight.shape[2]
    count = lax.axis_size("expert")
    me = lax.axis_index("expert")
    experts, _, units = gate_weight.shape
    bf16, f32 = jnp.bfloat16, jnp.float32
    fresh = jnp.transpose(jnp.stack([new_keys, new_values]), (0, 2, 3, 1, 4))
    fresh = jnp.pad(fresh, ((0, 0), (0, 0), (0, 0), (0, length - cached - steps), (0, 0)))
    share = route_weights / jnp.sum(route_weights, axis=-1, keepdims=True)
    hits = route_ids[..., None] == jnp.arange(128, dtype=jnp.int32)
    mix = jnp.sum(jnp.where(hits, share[..., None], 0.0), axis=2).reshape(rows, 128)
    lanes = jnp.arange(128, dtype=jnp.int32)[None, :] - me * toks
    counts = jnp.sum(
        jnp.where(
            lanes == jnp.arange(toks, dtype=jnp.int32)[:, None],
            ancestor_counts.astype(f32)[:, None],
            0.0,
        ),
        axis=0,
        keepdims=True,
    )
    table = jnp.concatenate(
        [
            jnp.pad(mix, ((0, padded_rows - rows), (0, 0))),
            jnp.pad(counts, ((0, 7), (0, 0))),
        ],
        axis=0,
    )
    dims = (steps, toks, key_heads, cached, count * toks, half)
    vmem = pl.BlockSpec(memory_space=pltpu.VMEM)
    hbm = pl.BlockSpec(memory_space=pl.ANY)
    dma = pltpu.SemaphoreType.DMA
    width = half // CHUNKS
    return pl.pallas_call(
        functools.partial(step_kernel, dims),
        out_shape=(
            jax.ShapeDtypeStruct(hidden_in.shape, bf16),
            jax.ShapeDtypeStruct((toks, key_heads, cached + steps, head_width), bf16),
            jax.ShapeDtypeStruct((toks, key_heads, cached + steps, head_width), bf16),
        ),
        in_specs=[vmem] * 7 + [hbm] * 3,
        out_specs=(vmem, vmem, vmem),
        scratch_shapes=[
            pltpu.VMEM((2, toks, key_heads, length, head_width), bf16),
            pltpu.VMEM((rows * query_heads, head_width), f32),
            pltpu.VMEM((2, padded_rows, 128), f32),
            pltpu.VMEM((2, count, padded_rows, half), bf16),
            pltpu.VMEM((count, padded_rows + 8, 128), f32),
            pltpu.VMEM(gate_weight.shape, bf16),
            pltpu.VMEM(up_weight.shape, bf16),
            pltpu.VMEM(down_weight.shape, bf16),
            pltpu.VMEM((2, experts, count * padded_rows, units), bf16),
            pltpu.VMEM((CHUNKS, count, padded_rows, width), bf16),
            pltpu.VMEM((CHUNKS, count, padded_rows, width), bf16),
            pltpu.VMEM((2, padded_rows, half), bf16),
            pltpu.VMEM((2, 2, REACH, key_heads, length, head_width), bf16),
            dma((3,)),
            dma((2,)),
            dma((count,)),
            dma((count,)),
            dma((count,)),
            dma((count,)),
            dma((count,)),
            dma((count,)),
            dma((2, experts)),
            dma((CHUNKS, count)),
            dma((CHUNKS, count)),
            dma((2,)),
            dma((2, 2)),
        ],
        compiler_params=pltpu.CompilerParams(
            collective_id=0, has_side_effects=True, vmem_limit_bytes=48 * 2**20
        ),
        name="step_kernel",
    )(
        hidden_in,
        queries,
        fresh,
        cache_keys,
        cache_values,
        table,
        norm_gain[None, :],
        gate_weight,
        up_weight,
        down_weight,
    )


def solution(mesh):
    fits = mesh.shape["group"] == 1 and mesh.shape["tensor"] == 2
    shards = one_group_shards if fits else grouped_shards
    in_specs = (
        P(None, ("parts", "expert", "group"), None),
        P(None, ("parts", "expert", "group"), "tensor", None),
        P(None, ("parts", "expert", "group"), "tensor", None),
        P(None, ("parts", "expert", "group"), "tensor", None),
        P(("parts", "expert", "group"), "tensor", None, None),
        P(("parts", "expert", "group"), "tensor", None, None),
        P(None, ("parts", "expert", "group"), None),
        P(None, ("parts", "expert", "group"), None),
        P(),
        P("expert", "group", "tensor"),
        P("expert", "group", "tensor"),
        P("expert", None, ("group", "tensor")),
        P(("parts", "expert", "group")),
    )
    out_specs = (
        P(None, ("parts", "expert", "group"), None),
        P(("parts", "expert", "group"), "tensor", None, None),
        P(("parts", "expert", "group"), "tensor", None, None),
    )
    return jax.shard_map(shards, mesh=mesh, in_specs=in_specs, out_specs=out_specs, check_vma=False)
```
